256 devices in a mesh: grp: 8 (over y, core), dev: 32 (over z, x).
Axes of the slice: x: 4, y: 4, z: 8, core: 2. Of those that a mesh axis runs over, the one named last changes fastest.
Arguments:
- video_in: bfloat16 [4, 256, 256, 1024], P(None, ('grp', 'dev')), may hold values from -24 to 24
- space_gain: float32 [1024], replicated, may hold values from 0.25 to 1.75
- space_project: bfloat16 [1024, 1536], replicated, may hold values from -6 to 6
- space_output: bfloat16 [512, 1024], replicated, may hold values from -0.25 to 0.25
- time_gain: float32 [1024], replicated, may hold values from 0.25 to 1.75
- time_project: bfloat16 [1024, 1536], replicated, may hold values from -6 to 6
- time_output: bfloat16 [512, 1024], replicated, may hold values from -0.25 to 0.25
Outputs:
- video_out: bfloat16 [4, 256, 256, 1024], P(None, ('grp', 'dev'))
The draws below stay inside these ranges and needn't reach their ends.
All inputs are finite; a program needn't handle non-finite values.
Results may differ from the reference program's by a relative error of at most 0.007.
Values may be sent and summed in bfloat16 or wider, within the bound.
A program may use at most 128 MiB of HBM per device.

```python
from functools import partial
import jax
import jax.numpy as jnp
from jax import lax

D = 1024
HEADS = 8
HEAD_DIM = 64
PATCHES = 256
CLIPS = 4
FRAMES = 256


def clipped_normal(key, shape):
    return jnp.clip(jax.random.normal(key, shape, jnp.float32), -4.0, 4.0)


def drawn_draw(key):
    attn_width = HEADS * HEAD_DIM
    subkeys = jax.random.split(key, 1)
    entries_draw = clipped_normal(subkeys[0], (D, 3 * attn_width)) * D ** (-0.5)
    return jnp.clip(entries_draw, -6.0, 6.0)


def draw_space_project(key, part):
    return drawn_draw(jax.random.fold_in(key, 11)).astype(jnp.bfloat16)


def draw_time_project(key, part):
    return drawn_draw(jax.random.fold_in(key, 23)).astype(jnp.bfloat16)


def draw_video_in(key, part):
    subkeys = jax.random.split(jax.random.fold_in(key, 37), 1)
    full_shape = (CLIPS, FRAMES, PATCHES, D)
    entries_draw = clipped_normal(subkeys[0], full_shape)
    return jnp.clip(entries_draw, -24.0, 24.0).astype(jnp.bfloat16)


def noise(own_key, dims, deviation, most, dtype=jnp.bfloat16):
    drawn = deviation * jax.random.normal(own_key, dims, jnp.float32)
    return jnp.clip(drawn, min=-most, max=most).astype(dtype)


def setup_inputs(seed: int = 0) -> dict:
    key_of = jax.random.split(jax.random.key(seed), 8)
    video_in = draw_video_in(jax.random.fold_in(key_of[7], 71), 0)
    space_gain = jnp.clip(1.0 + 0.15 * jax.random.normal(key_of[1], (D,), jnp.float32), 0.25, 1.75)
    space_project = draw_space_project(jax.random.fold_in(key_of[7], 71), 0)
    space_output = noise(key_of[3], (HEADS * HEAD_DIM, D), (HEADS * HEAD_DIM) ** -0.5, 0.25)
    time_gain = jnp.clip(1.0 + 0.15 * jax.random.normal(key_of[4], (D,), jnp.float32), 0.25, 1.75)
    time_project = draw_time_project(jax.random.fold_in(key_of[7], 71), 0)
    time_output = noise(key_of[6], (HEADS * HEAD_DIM, D), (HEADS * HEAD_DIM) ** -0.5, 0.25)
    return dict(video_in=video_in, space_gain=space_gain, space_project=space_project, space_output=space_output, time_gain=time_gain, time_project=time_project, time_output=time_output)


norm_epsilon = 1e-06
masked_score = -1e+30

def layer_norm(activations, gain_vec):
    floats = activations.astype(jnp.float32)
    centre = lax.optimization_barrier(jnp.mean(floats, axis=-1, keepdims=True))
    spread = lax.optimization_barrier(jnp.mean(jnp.square(floats - centre), axis=-1, keepdims=True))
    return ((floats - centre) * lax.rsqrt(spread + norm_epsilon) * gain_vec).astype(jnp.bfloat16)

def soft_weights(scores, allowed):
    scores = jnp.where(allowed, scores, masked_score)
    top_score = lax.optimization_barrier(jnp.max(scores, axis=-1, keepdims=True))
    exponent = jnp.where(allowed, jnp.exp(scores - top_score), 0.0)
    row_total = lax.optimization_barrier(jnp.sum(exponent, axis=-1, keepdims=True))
    return (exponent / row_total).astype(jnp.bfloat16)

def spatial_frame(frame_in, space_gain, space_project, space_output):
    attn_width = HEADS * HEAD_DIM
    normed = layer_norm(frame_in, space_gain)
    projected = jnp.dot(normed.reshape(-1, D), space_project, preferred_element_type=jnp.float32)
    projected = projected.astype(jnp.bfloat16).reshape(CLIPS, PATCHES, 3, HEADS, HEAD_DIM)
    queries = projected[:, :, 0].astype(jnp.float32)
    keys_all = projected[:, :, 1].astype(jnp.float32)
    values_all = projected[:, :, 2].astype(jnp.float32)
    scores = jnp.einsum('cqhe,ckhe->chqk', queries, keys_all) * HEAD_DIM ** (-0.5)
    allowed = jnp.ones((PATCHES, PATCHES), jnp.bool_)
    weights = soft_weights(scores, allowed)
    context = jnp.einsum('chqk,ckhe->cqhe', weights.astype(jnp.float32), values_all).astype(jnp.bfloat16)
    update = jnp.dot(context.reshape(-1, attn_width), space_output, preferred_element_type=jnp.float32)
    return (frame_in.astype(jnp.float32) + update.reshape(CLIPS, PATCHES, D)).astype(jnp.bfloat16)

def temporal_patch(patch_in, time_gain, time_project, time_output):
    attn_width = HEADS * HEAD_DIM
    normed = layer_norm(patch_in, time_gain)
    projected = jnp.dot(normed.reshape(-1, D), time_project, preferred_element_type=jnp.float32)
    projected = projected.astype(jnp.bfloat16).reshape(CLIPS, FRAMES, 3, HEADS, HEAD_DIM)
    queries = projected[:, :, 0].astype(jnp.float32)
    keys_all = projected[:, :, 1].astype(jnp.float32)
    values_all = projected[:, :, 2].astype(jnp.float32)
    scores = jnp.einsum('cqhe,ckhe->chqk', queries, keys_all) * HEAD_DIM ** (-0.5)
    allowed = jnp.arange(FRAMES)[None, :] <= jnp.arange(FRAMES)[:, None]
    weights = soft_weights(scores, allowed)
    context = jnp.einsum('chqk,ckhe->cqhe', weights.astype(jnp.float32), values_all).astype(jnp.bfloat16)
    update = jnp.dot(context.reshape(-1, attn_width), time_output, preferred_element_type=jnp.float32)
    update_rows = update.astype(jnp.bfloat16).reshape(CLIPS, FRAMES, D)
    return (patch_in.astype(jnp.float32) + update_rows.astype(jnp.float32)).astype(jnp.bfloat16)

def reference(video_in, space_gain, space_project, space_output, time_gain, time_project, time_output):
    frames_first = jnp.moveaxis(video_in, 1, 0)
    spatial_fn = partial(spatial_frame, space_gain=space_gain, space_project=space_project, space_output=space_output)
    mixed_rows = lax.map(spatial_fn, frames_first)
    by_patch = jnp.transpose(mixed_rows, (2, 1, 0, 3))
    temporal_fn = partial(temporal_patch, time_gain=time_gain, time_project=time_project, time_output=time_output)
    result = lax.map(temporal_fn, by_patch)
    return jnp.transpose(result, (1, 2, 0, 3))
```

```python
import functools

import jax
import jax.numpy as jnp
from jax import lax
from jax.experimental import pallas as pl
from jax.experimental.pallas import tpu as pltpu
from jax.sharding import PartitionSpec as P

HEADS = 8
HEAD_DIM = 64
ATTN = HEADS * HEAD_DIM
CORES = 2
X_SIZE = 4
UNIT = 4

norm_epsilon = 1e-06
masked_score = -1e30
exp2_scale = HEAD_DIM ** (-0.5) * 1.4426950408889634
MESH = pl.DeviceIdType.MESH


def norm_rows(rows, gain):
    centre = jnp.mean(rows, axis=-1, keepdims=True)
    shifted = rows - centre
    spread = jnp.mean(shifted * shifted, axis=-1, keepdims=True)
    return shifted * lax.rsqrt(spread + norm_epsilon) * gain


def soft_context(scores, values):
    top = jnp.max(scores, axis=-1, keepdims=True)
    exponent = jnp.exp2((scores - top) * exp2_scale)
    total = jnp.sum(exponent, axis=-1, keepdims=True)
    context = jnp.dot(exponent.astype(jnp.bfloat16), values, preferred_element_type=jnp.float32)
    return context * (1.0 / total)


def scores_of(queries, keys):
    return lax.dot_general(
        queries, keys, (((1,), (1,)), ((), ())), preferred_element_type=jnp.float32
    )


def layer_kernel(
    dims,
    video_hbm, space_gain, space_project_hbm, space_output_hbm,
    time_gain, time_project_hbm, time_output_hbm,
    out_hbm,
    video, space_project, space_output, time_project, time_output,
    normed, space_q, space_kv, space_ctx, mixed, outgoing, incoming,
    wide, time_q, time_k, time_v, bias, ctx_wide, ctx_out, ctx_in, result,
    video_sem, weight_sem, send_sem, recv_sem, back_send_sem, back_recv_sem, out_sem,
):
    xs, ys, zs, cs = dims
    groups = ys * zs * cs
    devices = xs * groups
    clips = xs
    patches = groups * UNIT
    width = video.shape[-1]
    pairs = HEADS // 2
    grp = lax.axis_index("grp")
    dev = lax.axis_index("dev")
    y = grp // cs
    core = grp % cs
    z = dev // xs
    x = dev % xs
    kind = (x + y + z) % clips
    my_group = (z * ys + y) * cs + core

    barrier = pltpu.get_barrier_semaphore()

    def greet(k, carry):
        other_grp = (grp + k // (xs * zs)) % (ys * cs)
        other_dev = (dev + k % (xs * zs)) % (xs * zs)
        pl.semaphore_signal(
            barrier, inc=1, device_id=(other_grp, other_dev), device_id_type=MESH
        )
        return carry

    lax.fori_loop(1, devices, greet, 0)

    def video_copy(step):
        clip = (step + kind) % clips
        return pltpu.make_async_copy(
            video_hbm.at[clip, 0], video.at[step], video_sem.at[step]
        )

    weights = [
        pltpu.make_async_copy(space_project_hbm, space_project, weight_sem.at[0]),
        pltpu.make_async_copy(space_output_hbm, space_output, weight_sem.at[1]),
        pltpu.make_async_copy(time_project_hbm, time_project, weight_sem.at[2]),
        pltpu.make_async_copy(time_output_hbm, time_output, weight_sem.at[3]),
    ]
    video_copy(0).start()
    weights[0].start()
    weights[1].start()
    for step in range(1, clips):
        video_copy(step).start()
    weights[2].start()
    weights[3].start()

    block = min(32, patches)
    row_blocks = patches // block

    def displaced(step, j):
        turn = j % zs
        rest = j // zs
        half = (turn + 1) // 2
        dz = (zs // 2 + zs + jnp.where(turn % 2 == 1, -half, half)) % zs
        dy = rest % ys
        dc = rest // ys
        dx = (step + 2 * clips + zs * clips - dy - dz) % clips
        return dx, dy, dz, dc

    def send_step(step):
        def send(j, carry):
            dx, dy, dz, dc = displaced(step, j)
            there_x = (x + dx) % xs
            there_y = (y + dy) % ys
            there_z = (z + dz) % zs
            there_c = (core + dc) % cs
            group = (there_z * ys + there_y) * cs + there_c
            is_self = (dx == 0) & (dy == 0) & (dz == 0) & (dc == 0)

            @pl.when(is_self)
            def _():
                pltpu.make_async_copy(
                    outgoing.at[step, group], incoming.at[step, j], recv_sem.at[step]
                ).start()

            @pl.when(jnp.logical_not(is_self))
            def _():
                pltpu.make_async_remote_copy(
                    src_ref=outgoing.at[step, group],
                    dst_ref=incoming.at[step, j],
                    send_sem=send_sem.at[step],
                    recv_sem=recv_sem.at[step],
                    device_id=(there_y * cs + there_c, there_z * xs + there_x),
                    device_id_type=MESH,
                ).start()

            return carry

        lax.fori_loop(0, groups, send, 0)

    def send_back(step):
        def send(j, carry):
            dx, dy, dz, dc = displaced(step, j)
            there_x = (x + xs - dx) % xs
            there_y = (y + ys - dy) % ys
            there_z = (z + zs - dz) % zs
            there_c = (core + cs - dc) % cs
            is_self = (dx == 0) & (dy == 0) & (dz == 0) & (dc == 0)

            @pl.when(is_self)
            def _():
                pltpu.make_async_copy(
                    ctx_out.at[step, j], ctx_in.at[step, my_group], back_recv_sem.at[step]
                ).start()

            @pl.when(jnp.logical_not(is_self))
            def _():
                pltpu.make_async_remote_copy(
                    src_ref=ctx_out.at[step, j],
                    dst_ref=ctx_in.at[step, my_group],
                    send_sem=back_send_sem.at[step],
                    recv_sem=back_recv_sem.at[step],
                    device_id=(there_y * cs + there_c, there_z * xs + there_x),
                    device_id_type=MESH,
                ).start()

            return carry

        lax.fori_loop(0, groups, send, 0)

    low_half = lax.broadcasted_iota(jnp.int32, (1, 128), 1) < HEAD_DIM
    low_halves = lax.broadcasted_iota(jnp.int32, (1, ATTN), 1) % 128 < HEAD_DIM

    def spatial(step):
        video_copy(step).wait()

        def norm_block(b, carry):
            rows = pl.ds(pl.multiple_of(b * block, block), block)
            normed[rows, :] = norm_rows(
                video[step, rows, :].astype(jnp.float32), space_gain[...]
            ).astype(jnp.bfloat16)
            return carry

        lax.fori_loop(0, row_blocks, norm_block, 0)

        @pl.when(step == 0)
        def _():
            weights[0].wait()

        queries = jnp.dot(
            normed[...], space_project[:, :ATTN], preferred_element_type=jnp.float32
        )
        space_q[0] = jnp.where(low_halves, queries, 0.0).astype(jnp.bfloat16)
        space_q[1] = jnp.where(low_halves, 0.0, queries).astype(jnp.bfloat16)

        def project(t, carry):
            columns = pl.ds(pl.multiple_of(t * 256, 256), 256)
            there = pl.ds(pl.multiple_of(ATTN + t * 256, 256), 256)
            space_kv[:, columns] = jnp.dot(
                normed[...], space_project[:, there], preferred_element_type=jnp.float32
            ).astype(jnp.bfloat16)
            return carry

        lax.fori_loop(0, 2 * ATTN // 256, project, 0)

        def attend(pair, carry):
            lanes = pl.ds(pl.multiple_of(pair * 128, 128), 128)
            value_lanes = pl.ds(pl.multiple_of(ATTN + pair * 128, 128), 128)
            keys = space_kv[:, lanes]
            values = space_kv[:, value_lanes]
            low = soft_context(scores_of(space_q[0, :, lanes], keys), values)
            high = soft_context(scores_of(space_q[1, :, lanes], keys), values)
            space_ctx[:, lanes] = jnp.where(low_half, low, high).astype(jnp.bfloat16)
            return carry

        lax.fori_loop(0, pairs, attend, 0)

        @pl.when(step == 0)
        def _():
            weights[1].wait()

        def finish(b, carry):
            rows = pl.ds(pl.multiple_of(b * block, block), block)
            update = jnp.dot(
                space_ctx[rows, :], space_output[...], preferred_element_type=jnp.float32
            )
            sums = (video[step, rows, :].astype(jnp.float32) + update).astype(jnp.bfloat16)
            mixed[step, rows, :] = sums
            after = norm_rows(sums.astype(jnp.float32), time_gain[...])
            there = pl.ds(pl.multiple_of(b * (block // UNIT), block // UNIT), block // UNIT)
            outgoing[step, there] = after.reshape(block // UNIT, UNIT, width).astype(
                jnp.bfloat16
            )
            return carry

        lax.fori_loop(0, row_blocks, finish, 0)

    def first_half(step, carry):
        spatial(step)

        @pl.when(step == 0)
        def _():
            pl.semaphore_wait(barrier, devices - 1)

        send_step(step)
        return carry

    lax.fori_loop(0, clips, first_half, 0)

    def frames(axis):
        slot = lax.broadcasted_iota(jnp.int32, (devices, devices), axis)
        step = slot // groups
        dx, dy, dz, dc = displaced(step, slot % groups)
        from_x = (x + xs - dx) % xs
        from_y = (y + ys - dy) % ys
        from_z = (z + zs - dz) % zs
        from_c = (core + cs - dc) % cs
        return ((from_y * cs + from_c) * zs + from_z) * xs + from_x

    bias[...] = jnp.where(frames(1) <= frames(0), 0.0, masked_score)

    weights[2].wait()
    weights[3].wait()

    def arrive(step, carry):
        pltpu.make_async_copy(incoming.at[step], incoming.at[step], recv_sem.at[step]).wait()
        flat = incoming[step].reshape(patches, width)
        normed[...] = flat

        def project(t, carry):
            columns = pl.ds(pl.multiple_of(t * 256, 256), 256)
            heads = jnp.dot(
                normed[...], time_project[:, columns], preferred_element_type=jnp.float32
            )
            wide[2 * t] = heads[:, :128]
            wide[2 * t + 1] = heads[:, 128:]
            return carry

        lax.fori_loop(0, 3 * ATTN // 256, project, 0)
        slots = pl.ds(pl.multiple_of(step * groups, groups), groups)
        for p in range(UNIT):
            mine = pl.ds(p, groups, stride=UNIT)
            for pair in range(pairs):
                lanes = pl.ds(pair * 128, 128)
                queries = wide[pair, mine, :]
                time_q[0, p, slots, lanes] = jnp.where(low_half, queries, 0.0).astype(jnp.bfloat16)
                time_q[1, p, slots, lanes] = jnp.where(low_half, 0.0, queries).astype(jnp.bfloat16)
                time_k[p, slots, lanes] = wide[pairs + pair, mine, :].astype(jnp.bfloat16)
                time_v[p, slots, lanes] = wide[2 * pairs + pair, mine, :].astype(jnp.bfloat16)
        return carry

    lax.fori_loop(0, clips, arrive, 0)

    def temporal(step, carry):
        slots = pl.ds(pl.multiple_of(step * groups, groups), groups)
        hidden = bias[slots, :]

        for p in range(UNIT):
            for pair in range(pairs):
                lanes = pl.ds(pair * 128, 128)
                keys = time_k[p, :, lanes]
                values = time_v[p, :, lanes]
                low = soft_context(scores_of(time_q[0, p, slots, lanes], keys) + hidden, values)
                high = soft_context(scores_of(time_q[1, p, slots, lanes], keys) + hidden, values)
                ctx_wide[pair, pl.ds(p, groups, stride=UNIT), :] = jnp.where(low_half, low, high)
        for pair in range(pairs):
            ctx_out[step, :, :, pl.ds(pair * 128, 128)] = (
                ctx_wide[pair].reshape(groups, UNIT, 128).astype(jnp.bfloat16)
            )
        send_back(step)
        return carry

    lax.fori_loop(0, clips, temporal, 0)

    def out_copy(step):
        clip = (step + kind) % clips
        return pltpu.make_async_copy(result.at[step], out_hbm.at[clip, 0], out_sem.at[step])

    def finish(step, carry):
        pltpu.make_async_copy(ctx_in.at[step], ctx_in.at[step], back_recv_sem.at[step]).wait()
        space_ctx[...] = ctx_in[step].reshape(patches, ATTN)

        def block_out(b, carry):
            rows = pl.ds(pl.multiple_of(b * block, block), block)
            update = jnp.dot(
                space_ctx[rows, :], time_output[...], preferred_element_type=jnp.float32
            ).astype(jnp.bfloat16)
            result[step, rows, :] = (
                mixed[step, rows, :].astype(jnp.float32) + update.astype(jnp.float32)
            ).astype(jnp.bfloat16)
            return carry

        lax.fori_loop(0, row_blocks, block_out, 0)
        out_copy(step).start()
        return carry

    lax.fori_loop(0, clips, finish, 0)

    for step in range(clips):
        sent = pl.ds(0, groups - 1 if step == 0 else groups)
        pltpu.make_async_copy(
            outgoing.at[step, sent], outgoing.at[step, sent], send_sem.at[step]
        ).wait()
        pltpu.make_async_copy(
            ctx_out.at[step, sent], ctx_out.at[step, sent], back_send_sem.at[step]
        ).wait()
        out_copy(step).wait()


def solution(mesh):
    group_count = mesh.shape["grp"]
    member_count = mesh.shape["dev"]
    dims = (X_SIZE, group_count // CORES, member_count // X_SIZE, CORES)

    def per_device(
        video_in, space_gain, space_project, space_output, time_gain, time_project, time_output
    ):
        clips, _, patches, width = video_in.shape
        groups = patches // UNIT
        frames = group_count * member_count
        bf16 = jnp.bfloat16
        anywhere = pl.BlockSpec(memory_space=pl.ANY)
        local = pl.BlockSpec(memory_space=pltpu.VMEM)
        dma = pltpu.SemaphoreType.DMA
        return pl.pallas_call(
            functools.partial(layer_kernel, dims),
            out_shape=jax.ShapeDtypeStruct(video_in.shape, bf16),
            in_specs=[anywhere, local, anywhere, anywhere, local, anywhere, anywhere],
            out_specs=anywhere,
            scratch_shapes=[
                pltpu.VMEM((clips, patches, width), bf16),
                pltpu.VMEM((width, 3 * ATTN), bf16),
                pltpu.VMEM((ATTN, width), bf16),
                pltpu.VMEM((width, 3 * ATTN), bf16),
                pltpu.VMEM((ATTN, width), bf16),
                pltpu.VMEM((patches, width), bf16),
                pltpu.VMEM((2, patches, ATTN), bf16),
                pltpu.VMEM((patches, 2 * ATTN), bf16),
                pltpu.VMEM((patches, ATTN), bf16),
                pltpu.VMEM((clips, patches, width), bf16),
                pltpu.VMEM((clips, groups, UNIT, width), bf16),
                pltpu.VMEM((clips, groups, UNIT, width), bf16),
                pltpu.VMEM((3 * ATTN // 128, patches, 128), jnp.float32),
                pltpu.VMEM((2, UNIT, frames, ATTN), bf16),
                pltpu.VMEM((UNIT, frames, ATTN), bf16),
                pltpu.VMEM((UNIT, frames, ATTN), bf16),
                pltpu.VMEM((frames, frames), jnp.float32),
                pltpu.VMEM((ATTN // 128, patches, 128), jnp.float32),
                pltpu.VMEM((clips, groups, UNIT, ATTN), bf16),
                pltpu.VMEM((clips, groups, UNIT, ATTN), bf16),
                pltpu.VMEM((clips, patches, width), bf16),
                dma((clips,)),
                dma((4,)),
                dma((clips,)),
                dma((clips,)),
                dma((clips,)),
                dma((clips,)),
                dma((clips,)),
            ],
            compiler_params=pltpu.CompilerParams(
                collective_id=0, has_side_effects=True, vmem_limit_bytes=60 * 1024 * 1024
            ),
            name="video_layer",
        )(
            video_in,
            space_gain.reshape(1, width),
            space_project,
            space_output,
            time_gain.reshape(1, width),
            time_project,
            time_output,
        )

    placed = P(None, ("grp", "dev"))
    return jax.shard_map(
        per_device,
        mesh=mesh,
        in_specs=(placed, P(), P(), P(), P(), P(), P()),
        out_specs=placed,
        check_vma=False,
    )
```

```python
import functools

import jax
import jax.numpy as jnp
from jax import lax
from jax.experimental import pallas as pl
from jax.experimental.pallas import tpu as pltpu
from jax.sharding import PartitionSpec as P

HEADS = 8
HEAD_DIM = 64
ATTN = HEADS * HEAD_DIM
CORES = 2
X_SIZE = 4
KINDS = 2
UNIT = KINDS

norm_epsilon = 1e-06
masked_score = -1e30
exp2_scale = HEAD_DIM ** (-0.5) * 1.4426950408889634
MESH = pl.DeviceIdType.MESH


def norm_rows(rows, gain):
    centre = jnp.mean(rows, axis=-1, keepdims=True)
    shifted = rows - centre
    spread = jnp.mean(shifted * shifted, axis=-1, keepdims=True)
    return shifted * lax.rsqrt(spread + norm_epsilon) * gain


def soft_context(scores, values):
    top = jnp.max(scores, axis=-1, keepdims=True)
    exponent = jnp.exp2((scores - top) * exp2_scale)
    total = jnp.sum(exponent, axis=-1, keepdims=True)
    context = jnp.dot(exponent.astype(jnp.bfloat16), values, preferred_element_type=jnp.float32)
    return context * (1.0 / total)


def scores_of(queries, keys):
    return lax.dot_general(
        queries, keys, (((1,), (1,)), ((), ())), preferred_element_type=jnp.float32
    )


def layer_kernel(
    dims,
    video_hbm, space_gain, space_project_hbm, space_output_hbm,
    time_gain, time_project_hbm, time_output_hbm,
    out_hbm,
    video, space_project, space_output, time_project, time_output,
    normed, space_q, space_kv, space_ctx, mixed, outgoing, incoming,
    wide, time_q, time_k, time_v, bias, ctx_wide, ctx_out, ctx_in, result,
    video_sem, weight_sem, send_sem, recv_sem, back_send_sem, back_recv_sem, out_sem,
):
    xs, ys, zs, cs = dims
    along = xs // KINDS
    groups = ys * zs * cs * along
    devices = KINDS * groups
    clips = video.shape[0]
    phases = clips // KINDS
    patches = groups * UNIT
    width = video.shape[-1]
    pairs = HEADS // 2
    grp = lax.axis_index("grp")
    dev = lax.axis_index("dev")
    y = grp // cs
    core = grp % cs
    z = dev // xs
    x = dev % xs
    kind = (x + y + z) % KINDS
    my_group = ((z * ys + y) * cs + core) * along + x // KINDS

    barrier = pltpu.get_barrier_semaphore()

    def clip_of(step):
        return step // KINDS * KINDS + (step + kind) % KINDS

    def video_copy(step):
        clip = clip_of(step)
        return pltpu.make_async_copy(
            video_hbm.at[clip, 0], video.at[step], video_sem.at[step]
        )

    weights = [
        pltpu.make_async_copy(space_project_hbm, space_project, weight_sem.at[0]),
        pltpu.make_async_copy(space_output_hbm, space_output, weight_sem.at[1]),
        pltpu.make_async_copy(time_project_hbm, time_project, weight_sem.at[2]),
        pltpu.make_async_copy(time_output_hbm, time_output, weight_sem.at[3]),
    ]
    video_copy(0).start()
    weights[0].start()
    weights[1].start()
    for step in range(1, clips):
        video_copy(step).start()
    weights[2].start()
    weights[3].start()

    def greet(k, carry):
        other_y = lax.rem(y + lax.rem(k, ys), ys)
        other_x = lax.rem(x + lax.div(k, ys), xs)
        for dz in range(zs):
            other_dev = lax.rem(z + dz, zs) * xs + other_x
            for dc in range(cs):
                other_grp = other_y * cs + lax.rem(core + dc, cs)

                @pl.when((k > 0) | (dz + dc > 0))
                def _():
                    pl.semaphore_signal(
                        barrier, inc=1, device_id=(other_grp, other_dev), device_id_type=MESH
                    )

        return carry

    lax.fori_loop(0, xs * ys, greet, 0)

    block = min(32, patches)
    row_blocks = patches // block

    turns = [zs // 2]
    for far in range(zs // 2 - 1, 0, -1):
        turns += [far, zs - far]
    turns += [0]
    rounds = groups // zs

    def displaced(step, rest, dz):
        dy = lax.rem(rest, ys)
        dc = lax.rem(lax.div(rest, ys), cs)
        far = lax.div(rest, ys * cs)
        dx = far * KINDS + lax.rem(step + ys * zs - dy - dz, KINDS)
        return dx, dy, dc

    def exchange(step, sign, local_copy, remote_copy):
        def one_round(rest, carry):
            for turn, dz in enumerate(turns):
                dx, dy, dc = displaced(step, rest, dz)
                there_x = lax.rem(x + xs + sign * dx, xs)
                there_y = lax.rem(y + ys + sign * dy, ys)
                there_z = lax.rem(z + zs + sign * dz, zs)
                there_c = lax.rem(core + cs + sign * dc, cs)
                group = ((there_z * ys + there_y) * cs + there_c) * along + lax.div(
                    there_x, KINDS
                )
                there = (there_y * cs + there_c, there_z * xs + there_x)
                j = rest * zs + turn
                if dz == 0:
                    is_self = (rest == 0) & (dx == 0)

                    @pl.when(is_self)
                    def _():
                        local_copy(j, group).start()

                    @pl.when(jnp.logical_not(is_self))
                    def _():
                        remote_copy(j, group, there).start()

                else:
                    remote_copy(j, group, there).start()
            return carry

        lax.fori_loop(0, rounds, one_round, 0)

    def send_step(step):
        exchange(
            step,
            1,
            lambda j, group: pltpu.make_async_copy(
                outgoing.at[step, group], incoming.at[step, j], recv_sem.at[step]
            ),
            lambda j, group, there: pltpu.make_async_remote_copy(
                src_ref=outgoing.at[step, group],
                dst_ref=incoming.at[step, j],
                send_sem=send_sem.at[step],
                recv_sem=recv_sem.at[step],
                device_id=there,
                device_id_type=MESH,
            ),
        )

    def send_back(step):
        exchange(
            step,
            -1,
            lambda j, group: pltpu.make_async_copy(
                ctx_out.at[step, j], ctx_in.at[step, my_group], back_recv_sem.at[step]
            ),
            lambda j, group, there: pltpu.make_async_remote_copy(
                src_ref=ctx_out.at[step, j],
                dst_ref=ctx_in.at[step, my_group],
                send_sem=back_send_sem.at[step],
                recv_sem=back_recv_sem.at[step],
                device_id=there,
                device_id_type=MESH,
            ),
        )

    low_half = lax.broadcasted_iota(jnp.int32, (1, 128), 1) < HEAD_DIM
    low_halves = lax.broadcasted_iota(jnp.int32, (1, ATTN), 1) % 128 < HEAD_DIM

    def spatial(step):
        video_copy(step).wait()

        def norm_block(b, carry):
            rows = pl.ds(pl.multiple_of(b * block, block), block)
            normed[rows, :] = norm_rows(
                video[step, rows, :].astype(jnp.float32), space_gain[...]
            ).astype(jnp.bfloat16)
            return carry

        lax.fori_loop(0, row_blocks, norm_block, 0)

        @pl.when(step == 0)
        def _():
            weights[0].wait()

        queries = jnp.dot(
            normed[...], space_project[:, :ATTN], preferred_element_type=jnp.float32
        )
        space_q[0] = jnp.where(low_halves, queries, 0.0).astype(jnp.bfloat16)
        space_q[1] = jnp.where(low_halves, 0.0, queries).astype(jnp.bfloat16)

        def project(t, carry):
            columns = pl.ds(pl.multiple_of(t * 256, 256), 256)
            there = pl.ds(pl.multiple_of(ATTN + t * 256, 256), 256)
            space_kv[:, columns] = jnp.dot(
                normed[...], space_project[:, there], preferred_element_type=jnp.float32
            ).astype(jnp.bfloat16)
            return carry

        lax.fori_loop(0, 2 * ATTN // 256, project, 0)

        def attend(pair, carry):
            lanes = pl.ds(pl.multiple_of(pair * 128, 128), 128)
            value_lanes = pl.ds(pl.multiple_of(ATTN + pair * 128, 128), 128)
            keys = space_kv[:, lanes]
            values = space_kv[:, value_lanes]
            low = soft_context(scores_of(space_q[0, :, lanes], keys), values)
            high = soft_context(scores_of(space_q[1, :, lanes], keys), values)
            space_ctx[:, lanes] = jnp.where(low_half, low, high).astype(jnp.bfloat16)
            return carry

        lax.fori_loop(0, pairs, attend, 0)

        @pl.when(step == 0)
        def _():
            weights[1].wait()

        def mix(t, carry):
            columns = pl.ds(pl.multiple_of(t * 256, 256), 256)
            update = jnp.dot(
                space_ctx[...], space_output[:, columns], preferred_element_type=jnp.float32
            )
            mixed[step, :, columns] = (
                video[step, :, columns].astype(jnp.float32) + update
            ).astype(jnp.bfloat16)
            return carry

        lax.fori_loop(0, width // 256, mix, 0)

        def finish(b, carry):
            rows = pl.ds(pl.multiple_of(b * block, block), block)
            after = norm_rows(mixed[step, rows, :].astype(jnp.float32), time_gain[...])
            there = pl.ds(pl.multiple_of(b * (block // UNIT), block // UNIT), block // UNIT)
            outgoing[step, there] = after.reshape(block // UNIT, UNIT, width).astype(
                jnp.bfloat16
            )
            return carry

        lax.fori_loop(0, row_blocks, finish, 0)

    def first_half(step, carry):
        spatial(step)

        @pl.when(step == 0)
        def _():
            pl.semaphore_wait(barrier, devices - 1)

        send_step(step)
        return carry

    lax.fori_loop(0, clips, first_half, 0)

    def frames(axis):
        slot = lax.broadcasted_iota(jnp.int32, (devices, devices), axis)
        turn = slot % zs
        half = (turn + 1) // 2
        dz = (zs // 2 + zs + jnp.where(turn % 2 == 1, -half, half)) % zs
        dx, dy, dc = displaced(slot // groups, slot % groups // zs, dz)
        from_x = (x + xs - dx) % xs
        from_y = (y + ys - dy) % ys
        from_z = (z + zs - dz) % zs
        from_c = (core + cs - dc) % cs
        return ((from_y * cs + from_c) * zs + from_z) * xs + from_x

    bias[...] = jnp.where(frames(1) <= frames(0), 0.0, masked_score)

    weights[2].wait()
    weights[3].wait()

    def arrive(phase, k):
        step = phase * KINDS + k
        pltpu.make_async_copy(incoming.at[step], incoming.at[step], recv_sem.at[step]).wait()
        flat = incoming[step].reshape(patches, width)
        normed[...] = flat

        def project(t, carry):
            columns = pl.ds(pl.multiple_of(t * 256, 256), 256)
            heads = jnp.dot(
                normed[...], time_project[:, columns], preferred_element_type=jnp.float32
            )
            wide[2 * t] = heads[:, :128]
            wide[2 * t + 1] = heads[:, 128:]
            return carry

        lax.fori_loop(0, 3 * ATTN // 256, project, 0)
        slots = pl.ds(pl.multiple_of(k * groups, groups), groups)
        for p in range(UNIT):
            mine = pl.ds(p, groups, stride=UNIT)
            for pair in range(pairs):
                lanes = pl.ds(pair * 128, 128)
                queries = wide[pair, mine, :]
                time_q[p, 0, slots, lanes] = jnp.where(low_half, queries, 0.0).astype(jnp.bfloat16)
                time_q[p, 1, slots, lanes] = jnp.where(low_half, 0.0, queries).astype(jnp.bfloat16)
                time_k[p, slots, lanes] = wide[pairs + pair, mine, :].astype(jnp.bfloat16)
                time_v[p, slots, lanes] = wide[2 * pairs + pair, mine, :].astype(jnp.bfloat16)

    def temporal(phase, k):
        step = phase * KINDS + k
        slots = pl.ds(pl.multiple_of(k * groups, groups), groups)

        for p in range(UNIT):
            for pair in range(pairs):
                lanes = pl.ds(pair * 128, 128)
                keys = time_k[p, :, lanes]
                values = time_v[p, :, lanes]
                queries = time_q[p, :, slots, lanes].reshape(2 * groups, 128)
                scores = scores_of(queries, keys).reshape(2, groups, devices)
                scores = (scores + bias[slots, :][None]).reshape(2 * groups, devices)
                both = soft_context(scores, values)
                ctx_wide[pair, pl.ds(p, groups, stride=UNIT), :] = jnp.where(
                    low_half, both[:groups], both[groups:]
                )
        for pair in range(pairs):
            ctx_out[step, :, :, pl.ds(pair * 128, 128)] = (
                ctx_wide[pair].reshape(groups, UNIT, 128).astype(jnp.bfloat16)
            )
        send_back(step)

    def second_half(phase, carry):
        def take(k, inner):
            arrive(phase, k)
            return inner

        lax.fori_loop(0, KINDS, take, 0)

        def give(k, inner):
            temporal(phase, k)
            return inner

        lax.fori_loop(0, KINDS, give, 0)
        return carry

    lax.fori_loop(0, phases, second_half, 0)

    def out_copy(step):
        clip = clip_of(step)
        return pltpu.make_async_copy(result.at[step], out_hbm.at[clip, 0], out_sem.at[step])

    def finish(step, carry):
        pltpu.make_async_copy(ctx_in.at[step], ctx_in.at[step], back_recv_sem.at[step]).wait()
        space_ctx[...] = ctx_in[step].reshape(patches, ATTN)

        def block_out(t, carry):
            columns = pl.ds(pl.multiple_of(t * 256, 256), 256)
            update = jnp.dot(
                space_ctx[...], time_output[:, columns], preferred_element_type=jnp.float32
            ).astype(jnp.bfloat16)
            result[step, :, columns] = (
                mixed[step, :, columns].astype(jnp.float32) + update.astype(jnp.float32)
            ).astype(jnp.bfloat16)
            return carry

        lax.fori_loop(0, width // 256, block_out, 0)
        out_copy(step).start()
        return carry

    lax.fori_loop(0, clips, finish, 0)

    for step in range(clips):
        sent = pl.ds(0, groups - 1 if step % KINDS == 0 else groups)
        pltpu.make_async_copy(
            outgoing.at[step, sent], outgoing.at[step, sent], send_sem.at[step]
        ).wait()
        pltpu.make_async_copy(
            ctx_out.at[step, sent], ctx_out.at[step, sent], back_send_sem.at[step]
        ).wait()
        out_copy(step).wait()


def solution(mesh):
    group_count = mesh.shape["grp"]
    member_count = mesh.shape["dev"]
    dims = (X_SIZE, group_count // CORES, member_count // X_SIZE, CORES)

    def per_device(
        video_in, space_gain, space_project, space_output, time_gain, time_project, time_output
    ):
        clips, _, patches, width = video_in.shape
        groups = patches // UNIT
        frames = group_count * member_count
        bf16 = jnp.bfloat16
        anywhere = pl.BlockSpec(memory_space=pl.ANY)
        local = pl.BlockSpec(memory_space=pltpu.VMEM)
        dma = pltpu.SemaphoreType.DMA
        return pl.pallas_call(
            functools.partial(layer_kernel, dims),
            out_shape=jax.ShapeDtypeStruct(video_in.shape, bf16),
            in_specs=[anywhere, local, anywhere, anywhere, local, anywhere, anywhere],
            out_specs=anywhere,
            scratch_shapes=[
                pltpu.VMEM((clips, patches, width), bf16),
                pltpu.VMEM((width, 3 * ATTN), bf16),
                pltpu.VMEM((ATTN, width), bf16),
                pltpu.VMEM((width, 3 * ATTN), bf16),
                pltpu.VMEM((ATTN, width), bf16),
                pltpu.VMEM((patches, width), bf16),
                pltpu.VMEM((2, patches, ATTN), bf16),
                pltpu.VMEM((patches, 2 * ATTN), bf16),
                pltpu.VMEM((patches, ATTN), bf16),
                pltpu.VMEM((clips, patches, width), bf16),
                pltpu.VMEM((clips, groups, UNIT, width), bf16),
                pltpu.VMEM((clips, groups, UNIT, width), bf16),
                pltpu.VMEM((3 * ATTN // 128, patches, 128), jnp.float32),
                pltpu.VMEM((UNIT, 2, frames, ATTN), bf16),
                pltpu.VMEM((UNIT, frames, ATTN), bf16),
                pltpu.VMEM((UNIT, frames, ATTN), bf16),
                pltpu.VMEM((frames, frames), jnp.float32),
                pltpu.VMEM((ATTN // 128, patches, 128), jnp.float32),
                pltpu.VMEM((clips, groups, UNIT, ATTN), bf16),
                pltpu.VMEM((clips, groups, UNIT, ATTN), bf16),
                pltpu.VMEM((clips, patches, width), bf16),
                dma((clips,)),
                dma((4,)),
                dma((clips,)),
                dma((clips,)),
                dma((clips,)),
                dma((clips,)),
                dma((clips,)),
            ],
            compiler_params=pltpu.CompilerParams(
                collective_id=0, has_side_effects=True, vmem_limit_bytes=60 * 1024 * 1024
            ),
            name="video_layer",
        )(
            video_in,
            space_gain.reshape(1, width),
            space_project,
            space_output,
            time_gain.reshape(1, width),
            time_project,
            time_output,
        )

    placed = P(None, ("grp", "dev"))
    return jax.shard_map(
        per_device,
        mesh=mesh,
        in_specs=(placed, P(), P(), P(), P(), P(), P()),
        out_specs=placed,
        check_vma=False,
    )
```

```python
import functools

import jax
import jax.numpy as jnp
from jax import lax
from jax.experimental import pallas as pl
from jax.experimental.pallas import tpu as pltpu
from jax.sharding import PartitionSpec as P

HEADS = 8
HEAD_DIM = 64
ATTN = HEADS * HEAD_DIM
CORES = 2
X_SIZE = 4
KINDS = 2
UNIT = KINDS

norm_epsilon = 1e-06
masked_score = -1e30
exp2_scale = HEAD_DIM ** (-0.5) * 1.4426950408889634
MESH = pl.DeviceIdType.MESH


def norm_rows(rows, gain):
    centre = jnp.mean(rows, axis=-1, keepdims=True)
    shifted = rows - centre
    spread = jnp.mean(shifted * shifted, axis=-1, keepdims=True)
    return shifted * lax.rsqrt(spread + norm_epsilon) * gain


def soft_context(scores, values):
    top = jnp.max(scores, axis=-1, keepdims=True)
    exponent = jnp.exp2((scores - top) * exp2_scale)
    beside = jnp.concatenate([values, jnp.ones_like(values)], axis=1)
    both = jnp.dot(exponent.astype(jnp.bfloat16), beside, preferred_element_type=jnp.float32)
    lanes = values.shape[1]
    return both[:, :lanes] * (1.0 / both[:, lanes:])


def scores_of(queries, keys):
    return lax.dot_general(
        queries, keys, (((1,), (1,)), ((), ())), preferred_element_type=jnp.float32
    )


def layer_kernel(
    dims,
    video_hbm, space_gain, space_project_hbm, space_output_hbm,
    time_gain, time_project_hbm, time_output_hbm,
    out_hbm,
    video, space_project, space_output, time_project, time_output,
    normed, space_q, space_kv, space_ctx, mixed, outgoing, incoming,
    wide, time_q, time_k, time_v, bias, ctx_wide, ctx_out, ctx_in, result,
    video_sem, weight_sem, send_sem, recv_sem, back_send_sem, back_recv_sem, out_sem,
):
    xs, ys, zs, cs = dims
    along = xs // KINDS
    groups = ys * zs * cs * along
    devices = KINDS * groups
    clips = video.shape[0]
    phases = clips // KINDS
    patches = groups * UNIT
    width = video.shape[-1]
    pairs = HEADS // 2
    grp = lax.axis_index("grp")
    dev = lax.axis_index("dev")
    y = grp // cs
    core = grp % cs
    z = dev // xs
    x = dev % xs
    kind = (x + y + z) % KINDS
    my_group = ((z * ys + y) * cs + core) * along + x // KINDS

    barrier = pltpu.get_barrier_semaphore()

    def clip_of(step):
        return step // KINDS * KINDS + (step + kind) % KINDS

    def video_copy(step):
        clip = clip_of(step)
        return pltpu.make_async_copy(
            video_hbm.at[clip, 0], video.at[step], video_sem.at[step]
        )

    weights = [
        pltpu.make_async_copy(space_project_hbm, space_project, weight_sem.at[0]),
        pltpu.make_async_copy(space_output_hbm, space_output, weight_sem.at[1]),
        pltpu.make_async_copy(time_project_hbm, time_project, weight_sem.at[2]),
        pltpu.make_async_copy(time_output_hbm, time_output, weight_sem.at[3]),
    ]
    video_copy(0).start()
    weights[0].start()
    weights[1].start()
    for step in range(1, clips):
        video_copy(step).start()
    weights[2].start()
    weights[3].start()

    def greet(k, carry):
        other_y = lax.rem(y + lax.rem(k, ys), ys)
        other_x = lax.rem(x + lax.div(k, ys), xs)
        for dz in range(zs):
            other_dev = lax.rem(z + dz, zs) * xs + other_x
            for dc in range(cs):
                other_grp = other_y * cs + lax.rem(core + dc, cs)

                @pl.when((k > 0) | (dz + dc > 0))
                def _():
                    pl.semaphore_signal(
                        barrier, inc=1, device_id=(other_grp, other_dev), device_id_type=MESH
                    )

        return carry

    lax.fori_loop(0, xs * ys, greet, 0)

    block = min(32, patches)
    row_blocks = patches // block

    turns = [zs // 2]
    for far in range(zs // 2 - 1, 0, -1):
        turns += [far, zs - far]
    turns += [0]
    rounds = groups // zs

    def displaced(step, rest, dz):
        dy = lax.rem(rest, ys)
        dc = lax.rem(lax.div(rest, ys), cs)
        far = lax.div(rest, ys * cs)
        dx = far * KINDS + lax.rem(step + ys * zs - dy - dz, KINDS)
        return dx, dy, dc

    def exchange(step, sign, local_copy, remote_copy):
        def one_round(rest, carry):
            for turn, dz in enumerate(turns):
                dx, dy, dc = displaced(step, rest, dz)
                there_x = lax.rem(x + xs + sign * dx, xs)
                there_y = lax.rem(y + ys + sign * dy, ys)
                there_z = lax.rem(z + zs + sign * dz, zs)
                there_c = lax.rem(core + cs + sign * dc, cs)
                group = ((there_z * ys + there_y) * cs + there_c) * along + lax.div(
                    there_x, KINDS
                )
                there = (there_y * cs + there_c, there_z * xs + there_x)
                j = rest * zs + turn
                if dz == 0:
                    is_self = (rest == 0) & (dx == 0)

                    @pl.when(is_self)
                    def _():
                        local_copy(j, group).start()

                    @pl.when(jnp.logical_not(is_self))
                    def _():
                        remote_copy(j, group, there).start()

                else:
                    remote_copy(j, group, there).start()
            return carry

        lax.fori_loop(0, rounds, one_round, 0)

    def send_step(step):
        exchange(
            step,
            1,
            lambda j, group: pltpu.make_async_copy(
                outgoing.at[step, group], incoming.at[step, j], recv_sem.at[step]
            ),
            lambda j, group, there: pltpu.make_async_remote_copy(
                src_ref=outgoing.at[step, group],
                dst_ref=incoming.at[step, j],
                send_sem=send_sem.at[step],
                recv_sem=recv_sem.at[step],
                device_id=there,
                device_id_type=MESH,
            ),
        )

    def send_back(step):
        exchange(
            step,
            -1,
            lambda j, group: pltpu.make_async_copy(
                ctx_out.at[step, j], ctx_in.at[step, my_group], back_recv_sem.at[step]
            ),
            lambda j, group, there: pltpu.make_async_remote_copy(
                src_ref=ctx_out.at[step, j],
                dst_ref=ctx_in.at[step, my_group],
                send_sem=back_send_sem.at[step],
                recv_sem=back_recv_sem.at[step],
                device_id=there,
                device_id_type=MESH,
            ),
        )

    low_half = lax.broadcasted_iota(jnp.int32, (1, 128), 1) < HEAD_DIM
    low_halves = lax.broadcasted_iota(jnp.int32, (1, ATTN), 1) % 128 < HEAD_DIM

    def spatial(step):
        video_copy(step).wait()

        def norm_block(b, carry):
            rows = pl.ds(pl.multiple_of(b * block, block), block)
            normed[rows, :] = norm_rows(
                video[step, rows, :].astype(jnp.float32), space_gain[...]
            ).astype(jnp.bfloat16)
            return carry

        lax.fori_loop(0, row_blocks, norm_block, 0, unroll=4)

        @pl.when(step == 0)
        def _():
            weights[0].wait()

        queries = jnp.dot(
            normed[...], space_project[:, :ATTN], preferred_element_type=jnp.float32
        )
        space_q[0] = jnp.where(low_halves, queries, 0.0).astype(jnp.bfloat16)
        space_q[1] = jnp.where(low_halves, 0.0, queries).astype(jnp.bfloat16)

        def project(t, carry):
            columns = pl.ds(pl.multiple_of(t * 256, 256), 256)
            there = pl.ds(pl.multiple_of(ATTN + t * 256, 256), 256)
            space_kv[:, columns] = jnp.dot(
                normed[...], space_project[:, there], preferred_element_type=jnp.float32
            ).astype(jnp.bfloat16)
            return carry

        lax.fori_loop(0, 2 * ATTN // 256, project, 0, unroll=2)

        def attend(pair, carry):
            lanes = pl.ds(pl.multiple_of(pair * 128, 128), 128)
            value_lanes = pl.ds(pl.multiple_of(ATTN + pair * 128, 128), 128)
            keys = space_kv[:, lanes]
            values = space_kv[:, value_lanes]
            low = soft_context(scores_of(space_q[0, :, lanes], keys), values)
            high = soft_context(scores_of(space_q[1, :, lanes], keys), values)
            space_ctx[:, lanes] = jnp.where(low_half, low, high).astype(jnp.bfloat16)
            return carry

        lax.fori_loop(0, pairs, attend, 0, unroll=4)

        @pl.when(step == 0)
        def _():
            weights[1].wait()

        def mix(t, carry):
            columns = pl.ds(pl.multiple_of(t * 256, 256), 256)
            update = jnp.dot(
                space_ctx[...], space_output[:, columns], preferred_element_type=jnp.float32
            )
            mixed[step, :, columns] = (
                video[step, :, columns].astype(jnp.float32) + update
            ).astype(jnp.bfloat16)
            return carry

        lax.fori_loop(0, width // 256, mix, 0, unroll=2)

        def finish(b, carry):
            rows = pl.ds(pl.multiple_of(b * block, block), block)
            after = norm_rows(mixed[step, rows, :].astype(jnp.float32), time_gain[...])
            there = pl.ds(pl.multiple_of(b * (block // UNIT), block // UNIT), block // UNIT)
            outgoing[step, there] = after.reshape(block // UNIT, UNIT, width).astype(
                jnp.bfloat16
            )
            return carry

        lax.fori_loop(0, row_blocks, finish, 0, unroll=4)

    def first_half(step, carry):
        spatial(step)

        @pl.when(step == 0)
        def _():
            pl.semaphore_wait(barrier, devices - 1)

        send_step(step)
        return carry

    lax.fori_loop(0, clips, first_half, 0)

    def frames(axis):
        slot = lax.broadcasted_iota(jnp.int32, (devices, devices), axis)
        turn = slot % zs
        half = (turn + 1) // 2
        dz = (zs // 2 + zs + jnp.where(turn % 2 == 1, -half, half)) % zs
        dx, dy, dc = displaced(slot // groups, slot % groups // zs, dz)
        from_x = (x + xs - dx) % xs
        from_y = (y + ys - dy) % ys
        from_z = (z + zs - dz) % zs
        from_c = (core + cs - dc) % cs
        return ((from_y * cs + from_c) * zs + from_z) * xs + from_x

    bias[...] = jnp.where(frames(1) <= frames(0), 0.0, masked_score)

    weights[2].wait()
    weights[3].wait()

    def arrive(phase, k):
        step = phase * KINDS + k
        pltpu.make_async_copy(incoming.at[step], incoming.at[step], recv_sem.at[step]).wait()
        flat = incoming[step].reshape(patches, width)
        normed[...] = flat

        def project(t, carry):
            columns = pl.ds(pl.multiple_of(t * 256, 256), 256)
            heads = jnp.dot(
                normed[...], time_project[:, columns], preferred_element_type=jnp.float32
            )
            wide[2 * t] = heads[:, :128]
            wide[2 * t + 1] = heads[:, 128:]
            return carry

        lax.fori_loop(0, 3 * ATTN // 256, project, 0)
        slots = pl.ds(pl.multiple_of(k * groups, groups), groups)
        for p in range(UNIT):
            mine = pl.ds(p, groups, stride=UNIT)
            for pair in range(pairs):
                lanes = pl.ds(pair * 128, 128)
                queries = wide[pair, mine, :]
                time_q[p, 0, slots, lanes] = jnp.where(low_half, queries, 0.0).astype(jnp.bfloat16)
                time_q[p, 1, slots, lanes] = jnp.where(low_half, 0.0, queries).astype(jnp.bfloat16)
                time_k[p, slots, lanes] = wide[pairs + pair, mine, :].astype(jnp.bfloat16)
                time_v[p, slots, lanes] = wide[2 * pairs + pair, mine, :].astype(jnp.bfloat16)

    def temporal(phase, k):
        step = phase * KINDS + k
        slots = pl.ds(pl.multiple_of(k * groups, groups), groups)

        for p in range(UNIT):
            for pair in range(pairs):
                lanes = pl.ds(pair * 128, 128)
                keys = time_k[p, :, lanes]
                values = time_v[p, :, lanes]
                queries = time_q[p, :, slots, lanes].reshape(2 * groups, 128)
                scores = scores_of(queries, keys).reshape(2, groups, devices)
                scores = (scores + bias[slots, :][None]).reshape(2 * groups, devices)
                both = soft_context(scores, values)
                ctx_wide[pair, pl.ds(p, groups, stride=UNIT), :] = jnp.where(
                    low_half, both[:groups], both[groups:]
                )
        for pair in range(pairs):
            ctx_out[step, :, :, pl.ds(pair * 128, 128)] = (
                ctx_wide[pair].reshape(groups, UNIT, 128).astype(jnp.bfloat16)
            )
        send_back(step)

    def second_half(phase, carry):
        def take(k, inner):
            arrive(phase, k)
            return inner

        lax.fori_loop(0, KINDS, take, 0)

        def give(k, inner):
            temporal(phase, k)
            return inner

        lax.fori_loop(0, KINDS, give, 0)
        return carry

    lax.fori_loop(0, phases, second_half, 0)

    def out_copy(step):
        clip = clip_of(step)
        return pltpu.make_async_copy(result.at[step], out_hbm.at[clip, 0], out_sem.at[step])

    def finish(step, carry):
        pltpu.make_async_copy(ctx_in.at[step], ctx_in.at[step], back_recv_sem.at[step]).wait()
        space_ctx[...] = ctx_in[step].reshape(patches, ATTN)

        def block_out(t, carry):
            columns = pl.ds(pl.multiple_of(t * 256, 256), 256)
            update = jnp.dot(
                space_ctx[...], time_output[:, columns], preferred_element_type=jnp.float32
            ).astype(jnp.bfloat16)
            result[step, :, columns] = (
                mixed[step, :, columns].astype(jnp.float32) + update.astype(jnp.float32)
            ).astype(jnp.bfloat16)
            return carry

        lax.fori_loop(0, width // 256, block_out, 0)
        out_copy(step).start()
        return carry

    lax.fori_loop(0, clips, finish, 0)

    for step in range(clips):
        sent = pl.ds(0, groups - 1 if step % KINDS == 0 else groups)
        pltpu.make_async_copy(
            outgoing.at[step, sent], outgoing.at[step, sent], send_sem.at[step]
        ).wait()
        pltpu.make_async_copy(
            ctx_out.at[step, sent], ctx_out.at[step, sent], back_send_sem.at[step]
        ).wait()
        out_copy(step).wait()


def solution(mesh):
    group_count = mesh.shape["grp"]
    member_count = mesh.shape["dev"]
    dims = (X_SIZE, group_count // CORES, member_count // X_SIZE, CORES)

    def per_device(
        video_in, space_gain, space_project, space_output, time_gain, time_project, time_output
    ):
        clips, _, patches, width = video_in.shape
        groups = patches // UNIT
        frames = group_count * member_count
        bf16 = jnp.bfloat16
        anywhere = pl.BlockSpec(memory_space=pl.ANY)
        local = pl.BlockSpec(memory_space=pltpu.VMEM)
        dma = pltpu.SemaphoreType.DMA
        return pl.pallas_call(
            functools.partial(layer_kernel, dims),
            out_shape=jax.ShapeDtypeStruct(video_in.shape, bf16),
            in_specs=[anywhere, local, anywhere, anywhere, local, anywhere, anywhere],
            out_specs=anywhere,
            scratch_shapes=[
                pltpu.VMEM((clips, patches, width), bf16),
                pltpu.VMEM((width, 3 * ATTN), bf16),
                pltpu.VMEM((ATTN, width), bf16),
                pltpu.VMEM((width, 3 * ATTN), bf16),
                pltpu.VMEM((ATTN, width), bf16),
                pltpu.VMEM((patches, width), bf16),
                pltpu.VMEM((2, patches, ATTN), bf16),
                pltpu.VMEM((patches, 2 * ATTN), bf16),
                pltpu.VMEM((patches, ATTN), bf16),
                pltpu.VMEM((clips, patches, width), bf16),
                pltpu.VMEM((clips, groups, UNIT, width), bf16),
                pltpu.VMEM((clips, groups, UNIT, width), bf16),
                pltpu.VMEM((3 * ATTN // 128, patches, 128), jnp.float32),
                pltpu.VMEM((UNIT, 2, frames, ATTN), bf16),
                pltpu.VMEM((UNIT, frames, ATTN), bf16),
                pltpu.VMEM((UNIT, frames, ATTN), bf16),
                pltpu.VMEM((frames, frames), jnp.float32),
                pltpu.VMEM((ATTN // 128, patches, 128), jnp.float32),
                pltpu.VMEM((clips, groups, UNIT, ATTN), bf16),
                pltpu.VMEM((clips, groups, UNIT, ATTN), bf16),
                pltpu.VMEM((clips, patches, width), bf16),
                dma((clips,)),
                dma((4,)),
                dma((clips,)),
                dma((clips,)),
                dma((clips,)),
                dma((clips,)),
                dma((clips,)),
            ],
            compiler_params=pltpu.CompilerParams(
                collective_id=0, has_side_effects=True, vmem_limit_bytes=60 * 1024 * 1024
            ),
            name="video_layer",
        )(
            video_in,
            space_gain.reshape(1, width),
            space_project,
            space_output,
            time_gain.reshape(1, width),
            time_project,
            time_output,
        )

    placed = P(None, ("grp", "dev"))
    return jax.shard_map(
        per_device,
        mesh=mesh,
        in_specs=(placed, P(), P(), P(), P(), P(), P()),
        out_specs=placed,
        check_vma=False,
    )
```
